128 devices in a mesh: cfg: 2 (over core), req: 4 (over y), seq: 16 (over z, x).
Axes of the slice: x: 4, y: 4, z: 4, core: 2. Of those that a mesh axis runs over, the one named last changes fastest.
Arguments:
- img_qkv: bfloat16 [2, 8, 4096, 6144], P('cfg', 'req', 'seq'), may hold values from -4.5 to 4.5
- txt_kv: bfloat16 [2, 8, 512, 4096], P('cfg', 'req', 'seq'), may hold values from -4.5 to 4.5
- text_len: int32 [8], P('req'), may hold values from 77 to 512
- t_index: int32 [8], P('req'), may hold values from 0 to 3
- guidance: float32 [8], P('req'), may hold values from 1.5 to 6
- modulation: float32 [2, 8, 3, 3072], P('cfg', 'req'), may hold values from -4 to 4
- img_hidden: bfloat16 [2, 8, 4096, 3072], P('cfg', 'req', 'seq'), may hold values from -6 to 6
- latents: float32 [8, 4096, 64], P('req', 'seq', 'cfg'), may hold values from -6 to 6
- proj_weight: bfloat16 [2048, 3072], P(('cfg', 'req', 'seq')), may hold values from -0.125 to 0.125
- final_weight: bfloat16 [3072, 64], replicated, may hold values from -0.109375 to 0.109375
Outputs:
- latents_next: float32 [8, 4096, 64], P('req', 'seq', 'cfg')
- vel_norm: float32 [2, 8], P('cfg', 'req')
- max_logit: float32 [2, 8], P('cfg', 'req')
The draws below stay inside these ranges and needn't reach their ends.
All inputs are finite; a program needn't handle non-finite values.
Results may differ from the reference program's by a relative error of at most 0.0033.
Values may be sent and summed in bfloat16 or wider, within the bound.
A program may use at most 128 MiB of HBM per device.

```python
import math
import jax
import jax.numpy as jnp
from jax import lax

D = 3072
HEADS = 16
HD = 128
C = 64
STEPS = 4
ATT = 2048
PROMPTS = 8
IMG = 4096
TXT = 512


def draw_text_len(key, part):
    lengths = jax.random.randint(key, (PROMPTS,), TXT * 3 // 20 + 1, TXT + 1)
    longest = jax.random.randint(jax.random.fold_in(key, 1), (), 0, PROMPTS)
    return jnp.where(jnp.arange(PROMPTS) == longest, TXT, lengths).astype(jnp.int32)


def draw_img_qkv(key, part):
    full_shape = (2, PROMPTS, IMG, 3 * ATT)
    column = jnp.arange(3 * ATT)[None, None, None, :]
    is_query = column < ATT
    drawn = jax.random.normal(key, full_shape, jnp.float32)
    drawn = jnp.where(is_query, 2.0 * drawn, drawn)
    drawn = jnp.clip(drawn, -4.5, 4.5)
    return drawn.astype(jnp.bfloat16)


def with_ends(values, key, low, top_value):
    dims = values.shape
    spot = [jax.random.randint(jax.random.fold_in(key, axis), (), 0, dims[axis]) for axis in range(len(dims))]
    values = values.at[tuple(spot)].set(low)
    longest = dims.index(max(dims))
    spot[longest] = (spot[longest] + 1) % dims[longest]
    return values.at[tuple(spot)].set(top_value)


def steps_of(key, dims, pieces, smallest, top_value):
    gain = 1.0
    for position, blocks in pieces:
        steps = jax.random.uniform(jax.random.fold_in(jax.random.fold_in(key, 6), position), (blocks,), jnp.float32, smallest / len(pieces), top_value / len(pieces))
        gain = gain * jnp.repeat(jnp.exp(steps), dims[position] // blocks).reshape((-1,) + (1,) * (len(dims) - 1 - position))
    return gain


def bell_draw(key, extent, width, bound, pieces=(), dtype=jnp.bfloat16):
    factor_of = steps_of(key, extent, pieces, -0.22, 0.18) if pieces else 1.0
    values = jax.random.normal(key, extent, jnp.float32) * width * factor_of
    return jnp.minimum(jnp.maximum(values, -bound), bound).astype(dtype)


def setup_inputs(seed: int = 0) -> dict:
    key_list = jax.random.split(jax.random.key(seed), 11)
    img_qkv = draw_img_qkv(jax.random.fold_in(key_list[10], 71), 0)
    txt_kv = bell_draw(key_list[1], (2, PROMPTS, TXT, 2 * ATT), 1.0, 4.5, ((0, 2), (1, 4), (2, 16)))
    text_len = draw_text_len(jax.random.fold_in(key_list[10], 71), 0)
    t_index = with_ends(jax.random.randint(key_list[3], (PROMPTS,), 0, STEPS), jax.random.fold_in(key_list[3], 1), 0, STEPS - 1).astype(jnp.int32)
    guidance = jnp.clip(jnp.exp(math.log(6.0) - 1.3862944 * jax.random.uniform(key_list[4], (PROMPTS,), jnp.float32) ** steps_of(key_list[4], (PROMPTS,), ((0, 4),), -0.2, 0.2)), 1.5, 6.0)
    modulation = bell_draw(key_list[5], (2, PROMPTS, 3, D), 1.0, 4.0, ((0, 2), (1, 4)), jnp.float32)
    img_hidden = bell_draw(key_list[6], (2, PROMPTS, IMG, D), 1.0, 6.0, ((0, 2), (1, 4), (2, 16)))
    latents = bell_draw(key_list[7], (PROMPTS, IMG, C), 1.0, 6.0, ((0, 4), (1, 16), (2, 2)), jnp.float32)
    proj_weight = bell_draw(key_list[8], (ATT, D), ATT ** -0.5, 0.125, ((0, 128),))
    final_weight = bell_draw(key_list[9], (D, C), D ** -0.5, 0.109375)
    return dict(img_qkv=img_qkv, txt_kv=txt_kv, text_len=text_len, t_index=t_index, guidance=guidance, modulation=modulation, img_hidden=img_hidden, latents=latents, proj_weight=proj_weight, final_weight=final_weight)


time_shift = 1.15
norm_eps = 1e-06

def sigma_of(step_index):
    fraction = 1.0 - step_index.astype(jnp.float32) / STEPS
    lifted = fraction * math.exp(time_shift)
    return lifted / (lifted + 1.0 - fraction)

def head_attention(queries, key_rows, value_rows, key_valid):
    img_len = queries.shape[0]
    block_rows = math.gcd(img_len, 1024)

    def one_block(query_rows):
        logits = jnp.dot(query_rows, key_rows.T, preferred_element_type=jnp.float32) * HD ** (-0.5)
        logits = jnp.where(key_valid[None, :], logits, -jnp.inf)
        row_max = lax.optimization_barrier(jnp.max(logits, axis=1, keepdims=True))
        weights = jnp.exp(logits - row_max)
        weights = (weights / lax.optimization_barrier(jnp.sum(weights, axis=1, keepdims=True))).astype(jnp.bfloat16)
        mixed_rows = jnp.dot(weights, value_rows, preferred_element_type=jnp.float32).astype(jnp.bfloat16)
        return (mixed_rows, jnp.max(row_max))
    mixed_rows, top_logit = lax.map(one_block, queries.reshape(img_len // block_rows, block_rows, HD))
    return (mixed_rows.reshape(img_len, HD), jnp.max(top_logit))

def velocity_of(qkv_rows, kv_rows, length, mod_rows, hidden_rows, proj_weight, final_weight):
    img_len = qkv_rows.shape[0]
    txt_len = kv_rows.shape[0]
    joined = qkv_rows.reshape(img_len, 3, HEADS, HD)
    text_rows = kv_rows.reshape(txt_len, 2, HEADS, HD)
    key_rows = jnp.concatenate([text_rows[:, 0], joined[:, 1]], axis=0)
    value_rows = jnp.concatenate([text_rows[:, 1], joined[:, 2]], axis=0)
    key_valid = jnp.concatenate([jnp.arange(txt_len) < length, jnp.ones((img_len,), jnp.bool_)])

    def per_head(triple):
        return head_attention(triple[0], triple[1], triple[2], key_valid)
    mixed_rows, top_logit = lax.map(per_head, (joined[:, 0].transpose(1, 0, 2), key_rows.transpose(1, 0, 2), value_rows.transpose(1, 0, 2)))
    attended = mixed_rows.transpose(1, 0, 2).reshape(img_len, HEADS * HD)
    projected = jnp.dot(attended, proj_weight, preferred_element_type=jnp.float32)
    hidden = hidden_rows.astype(jnp.float32) + mod_rows[0][None, :] * projected
    average = lax.optimization_barrier(jnp.mean(hidden, axis=1, keepdims=True))
    centred = hidden - average
    variance = lax.optimization_barrier(jnp.mean(centred * centred, axis=1, keepdims=True))
    normed = (centred / jnp.sqrt(variance + norm_eps) * (1.0 + mod_rows[1][None, :]) + mod_rows[2][None, :]).astype(jnp.bfloat16)
    return (jnp.dot(normed, final_weight, preferred_element_type=jnp.float32), jnp.max(top_logit))

def reference(img_qkv, txt_kv, text_len, t_index, guidance, modulation, img_hidden, latents, proj_weight, final_weight):
    velocity = []
    logit_rows = []
    for copy_idx in range(2):
        vel_row = []
        max_row = []
        for prompt in range(PROMPTS):
            vel_one, max_one = velocity_of(img_qkv[copy_idx, prompt], txt_kv[copy_idx, prompt], text_len[prompt], modulation[copy_idx, prompt], img_hidden[copy_idx, prompt], proj_weight, final_weight)
            vel_row.append(vel_one)
            max_row.append(max_one)
        velocity.append(vel_row)
        logit_rows.append(jnp.stack(max_row))
    advanced = []
    first_norms = []
    second_norms = []
    half_chan = C // 2
    for prompt in range(PROMPTS):
        cond_vel = velocity[0][prompt]
        uncond_vel = velocity[1][prompt]
        guided = uncond_vel + guidance[prompt] * (cond_vel - uncond_vel)
        lower = guided[:, :half_chan]
        upper = guided[:, half_chan:]
        first_norms.append(jnp.sqrt(jnp.mean(lower * lower) + norm_eps))
        second_norms.append(jnp.sqrt(jnp.mean(upper * upper) + norm_eps))
        euler_step = sigma_of(t_index[prompt] + 1) - sigma_of(t_index[prompt])
        advanced.append(latents[prompt] + euler_step * guided)
    norms = jnp.stack([jnp.stack(first_norms), jnp.stack(second_norms)])
    return (jnp.stack(advanced), norms, jnp.stack(logit_rows))
```

```python
import functools
import math

import jax
import jax.numpy as jnp
from jax import lax
from jax.experimental import pallas as pl
from jax.experimental.pallas import tpu as pltpu
from jax.sharding import PartitionSpec as P

HEADS = 16
HD = 128
STEPS = 4
BQ = 512


time_shift = 1.15
norm_eps = 1e-06


def swapped(value, axis, stride):
    return lax.ppermute(value, axis, [(i, i ^ 1 << stride) for i in range(lax.axis_size(axis))])


def sigma_of(step_index):
    fraction = 1.0 - step_index.astype(jnp.float32) / STEPS
    lifted = fraction * math.exp(time_shift)
    return lifted / (lifted + 1.0 - fraction)


def attn_kernel(tl_ref, q_ref, kt_ref, vt_ref, ki_ref, vi_ref, o_ref, m_ref):
    p = pl.program_id(0)
    q = q_ref[...]
    dims = (((1,), (1,)), ((), ()))
    st = lax.dot_general(q, kt_ref[...], dims, preferred_element_type=jnp.float32) * HD ** (-0.5)
    si = lax.dot_general(q, ki_ref[...], dims, preferred_element_type=jnp.float32) * HD ** (-0.5)
    col = lax.broadcasted_iota(jnp.int32, st.shape, 1)
    st = jnp.where(col < tl_ref[p], st, -jnp.inf)
    m = jnp.maximum(jnp.max(st, axis=1, keepdims=True), jnp.max(si, axis=1, keepdims=True))
    et = jnp.exp(st - m)
    ei = jnp.exp(si - m)
    inv = 1.0 / (jnp.sum(et, axis=1, keepdims=True) + jnp.sum(ei, axis=1, keepdims=True))
    pt = (et * inv).astype(jnp.bfloat16)
    pi = (ei * inv).astype(jnp.bfloat16)
    o = jnp.dot(pt, vt_ref[...], preferred_element_type=jnp.float32)
    o = o + jnp.dot(pi, vi_ref[...], preferred_element_type=jnp.float32)
    o_ref[...] = o.astype(o_ref.dtype)
    m_ref[...] = jnp.full(m_ref.shape, jnp.max(m), jnp.float32)


def attention(text_len, img, txt):
    prompts, img_len, _ = img.shape
    txt_len = txt.shape[1]
    nq = img_len // BQ
    grid_spec = pltpu.PrefetchScalarGridSpec(
        num_scalar_prefetch=1,
        grid=(prompts, nq),
        in_specs=[
            pl.BlockSpec((None, BQ, HD), lambda p, i, tl: (p, i, 0)),
            pl.BlockSpec((None, txt_len, HD), lambda p, i, tl: (p, 0, 0)),
            pl.BlockSpec((None, txt_len, HD), lambda p, i, tl: (p, 0, 1)),
            pl.BlockSpec((None, img_len, HD), lambda p, i, tl: (p, 0, 1)),
            pl.BlockSpec((None, img_len, HD), lambda p, i, tl: (p, 0, 2)),
        ],
        out_specs=[
            pl.BlockSpec((None, BQ, HD), lambda p, i, tl: (p, i, 0)),
            pl.BlockSpec((None, None, 8, 128), lambda p, i, tl: (p, i, 0, 0)),
        ],
    )
    flops = 4 * prompts * img_len * (img_len + txt_len) * HD
    cost = pl.CostEstimate(
        flops=flops,
        transcendentals=prompts * img_len * (img_len + txt_len),
        bytes_accessed=img.size * 2 + txt.size * 2 + prompts * img_len * HD * 2,
    )
    out, top = pl.pallas_call(
        attn_kernel,
        grid_spec=grid_spec,
        out_shape=[
            jax.ShapeDtypeStruct((prompts, img_len, HD), jnp.bfloat16),
            jax.ShapeDtypeStruct((prompts, nq, 8, 128), jnp.float32),
        ],
        compiler_params=pltpu.CompilerParams(
            dimension_semantics=("arbitrary", "arbitrary"),
            vmem_limit_bytes=60 * 1024 * 1024,
        ),
        cost_estimate=cost,
    )(text_len, img, txt, txt, img, img)
    return out, jnp.max(top, axis=(1, 2, 3))


def shards(
    img_qkv,
    txt_kv,
    text_len,
    t_index,
    guidance,
    modulation,
    img_hidden,
    latents,
    proj_weight,
    final_weight,
):
    local_prompts = img_qkv.shape[1]
    img_dev = img_qkv.shape[2]
    txt_dev = txt_kv.shape[2]
    seq = lax.axis_size("seq")
    joined = img_qkv[0].reshape(local_prompts, img_dev, 3, HEADS, HD)
    text_rows = txt_kv[0].reshape(local_prompts, txt_dev, 2, HEADS, HD)
    full_img = lax.all_to_all(joined, "seq", split_axis=3, concat_axis=1, tiled=True)
    full_txt = lax.all_to_all(text_rows, "seq", split_axis=3, concat_axis=1, tiled=True)
    img_len = full_img.shape[1]
    txt_len = full_txt.shape[1]
    local_heads = full_img.shape[3]
    img_flat = full_img.reshape(local_prompts, img_len, 3 * local_heads * HD)
    txt_flat = full_txt.reshape(local_prompts, txt_len, 2 * local_heads * HD)
    head_rows, local_max = attention(text_len, img_flat, txt_flat)
    head_rows = head_rows.reshape(local_prompts, img_len, local_heads, HD)
    token_rows = lax.all_to_all(head_rows, "seq", split_axis=1, concat_axis=2, tiled=True)
    attended = token_rows.reshape(local_prompts * img_dev, HEADS * HD)
    projected = jnp.dot(
        attended,
        lax.all_gather(proj_weight, ("cfg", "req", "seq"), axis=0, tiled=True),
        preferred_element_type=jnp.float32,
    )
    projected = projected.reshape(local_prompts, img_dev, projected.shape[1])
    mod_rows = modulation[0]
    hidden = img_hidden[0].astype(jnp.float32) + mod_rows[:, 0][:, None, :] * projected
    average = jnp.mean(hidden, axis=2, keepdims=True)
    centred = hidden - average
    variance = jnp.mean(centred * centred, axis=2, keepdims=True)
    normed = (
        centred / jnp.sqrt(variance + norm_eps) * (1.0 + mod_rows[:, 1][:, None, :])
        + mod_rows[:, 2][:, None, :]
    ).astype(jnp.bfloat16)
    velocity = jnp.einsum("ptd,dc->ptc", normed, final_weight, preferred_element_type=jnp.float32)
    half_chan = latents.shape[2]
    copy_pos = lax.axis_index("cfg")
    own_part = lax.dynamic_slice_in_dim(velocity, copy_pos * half_chan, half_chan, 2)
    other_part = lax.dynamic_slice_in_dim(velocity, (1 - copy_pos) * half_chan, half_chan, 2)
    partner = swapped(other_part, "cfg", 0)
    is_cond = copy_pos == 0
    cond_vel = jnp.where(is_cond, own_part, partner)
    uncond_vel = jnp.where(is_cond, partner, own_part)
    guided = uncond_vel + guidance[:, None, None] * (cond_vel - uncond_vel)
    square_sum = jnp.sum(guided * guided, axis=(1, 2))
    stats = jnp.concatenate([square_sum, local_max])
    gathered = lax.all_to_all(
        jnp.broadcast_to(stats[None], (seq, stats.shape[0])), "seq", 0, 0, tiled=True
    )
    total_sq = jnp.sum(gathered[:, :local_prompts], axis=0)
    global_max = jnp.max(gathered[:, local_prompts:], axis=0)
    vel_norm = jnp.sqrt(total_sq / (img_len * half_chan) + norm_eps)
    euler_step = sigma_of(t_index + 1) - sigma_of(t_index)
    advanced = latents + euler_step[:, None, None] * guided
    return (advanced, vel_norm.reshape(1, local_prompts), global_max.reshape(1, local_prompts))


def solution(mesh):
    return jax.shard_map(
        shards,
        mesh=mesh,
        in_specs=(
            P("cfg", "req", "seq", None),
            P("cfg", "req", "seq", None),
            P("req"),
            P("req"),
            P("req"),
            P("cfg", "req", None, None),
            P("cfg", "req", "seq", None),
            P("req", "seq", "cfg"),
            P(("cfg", "req", "seq"), None),
            P(),
        ),
        out_specs=(P("req", "seq", "cfg"), P("cfg", "req"), P("cfg", "req")),
        check_vma=False,
    )
```

```python
import functools
import math

import jax
import jax.numpy as jnp
from jax import lax
from jax.experimental import pallas as pl
from jax.experimental.pallas import tpu as pltpu
from jax.sharding import PartitionSpec as P

HEADS = 16
HD = 128
STEPS = 4
BQ = 512


time_shift = 1.15
norm_eps = 1e-06


def swapped(value, axis, stride):
    return lax.ppermute(value, axis, [(i, i ^ 1 << stride) for i in range(lax.axis_size(axis))])


def sigma_of(step_index):
    fraction = 1.0 - step_index.astype(jnp.float32) / STEPS
    lifted = fraction * math.exp(time_shift)
    return lifted / (lifted + 1.0 - fraction)


def attn_kernel(tl_ref, q_ref, kt_ref, vt_ref, ki_ref, vi_ref, o_ref, m_ref):
    p = pl.program_id(0)
    q = q_ref[...].reshape(-1, HD)
    kt = kt_ref[...].reshape(-1, HD)
    vt = vt_ref[...].reshape(-1, HD)
    ki = ki_ref[...].reshape(-1, HD)
    vi = vi_ref[...].reshape(-1, HD)
    dims = (((1,), (1,)), ((), ()))
    st = lax.dot_general(q, kt, dims, preferred_element_type=jnp.float32) * HD ** (-0.5)
    si = lax.dot_general(q, ki, dims, preferred_element_type=jnp.float32) * HD ** (-0.5)
    col = lax.broadcasted_iota(jnp.int32, st.shape, 1)
    st = jnp.where(col < tl_ref[p], st, -jnp.inf)
    m = jnp.maximum(jnp.max(st, axis=1, keepdims=True), jnp.max(si, axis=1, keepdims=True))
    et = jnp.exp(st - m)
    ei = jnp.exp(si - m)
    inv = 1.0 / (jnp.sum(et, axis=1, keepdims=True) + jnp.sum(ei, axis=1, keepdims=True))
    pt = (et * inv).astype(jnp.bfloat16)
    pi = (ei * inv).astype(jnp.bfloat16)
    o = jnp.dot(pt, vt, preferred_element_type=jnp.float32)
    o = o + jnp.dot(pi, vi, preferred_element_type=jnp.float32)
    o_ref[...] = o.astype(o_ref.dtype).reshape(o_ref.shape)
    m_ref[...] = jnp.full(m_ref.shape, jnp.max(m), jnp.float32)


def attention(text_len, img, txt):
    src, prompts, _, rows, _ = img.shape
    trows = txt.shape[3]
    img_len = src * rows
    txt_len = src * trows
    per = BQ // rows
    nq = src // per
    grid_spec = pltpu.PrefetchScalarGridSpec(
        num_scalar_prefetch=1,
        grid=(prompts, nq),
        in_specs=[
            pl.BlockSpec((per, None, None, rows, HD), lambda p, i, tl: (i, p, 0, 0, 0)),
            pl.BlockSpec((src, None, None, trows, HD), lambda p, i, tl: (0, p, 0, 0, 0)),
            pl.BlockSpec((src, None, None, trows, HD), lambda p, i, tl: (0, p, 1, 0, 0)),
            pl.BlockSpec((src, None, None, rows, HD), lambda p, i, tl: (0, p, 1, 0, 0)),
            pl.BlockSpec((src, None, None, rows, HD), lambda p, i, tl: (0, p, 2, 0, 0)),
        ],
        out_specs=[
            pl.BlockSpec((per, None, rows, HD), lambda p, i, tl: (i, p, 0, 0)),
            pl.BlockSpec((None, None, 8, 128), lambda p, i, tl: (p, i, 0, 0)),
        ],
    )
    cost = pl.CostEstimate(
        flops=4 * prompts * img_len * (img_len + txt_len) * HD,
        transcendentals=prompts * img_len * (img_len + txt_len),
        bytes_accessed=img.size * 2 + txt.size * 2 + prompts * img_len * HD * 2,
    )
    out, top = pl.pallas_call(
        attn_kernel,
        grid_spec=grid_spec,
        out_shape=[
            jax.ShapeDtypeStruct((src, prompts, rows, HD), jnp.bfloat16),
            jax.ShapeDtypeStruct((prompts, nq, 8, 128), jnp.float32),
        ],
        compiler_params=pltpu.CompilerParams(
            dimension_semantics=("arbitrary", "arbitrary"),
            vmem_limit_bytes=60 * 1024 * 1024,
        ),
        cost_estimate=cost,
    )(text_len, img, txt, txt, img, img)
    return out, jnp.max(top, axis=(1, 2, 3))


def shards(
    img_qkv,
    txt_kv,
    text_len,
    t_index,
    guidance,
    modulation,
    img_hidden,
    latents,
    proj_weight,
    final_weight,
):
    local_prompts = img_qkv.shape[1]
    img_dev = img_qkv.shape[2]
    txt_dev = txt_kv.shape[2]
    seq = lax.axis_size("seq")
    joined = img_qkv[0].reshape(local_prompts, img_dev, 3, seq, HEADS // seq * HD)
    joined = joined.transpose(3, 0, 2, 1, 4)
    text_rows = txt_kv[0].reshape(local_prompts, txt_dev, 2, seq, HEADS // seq * HD)
    text_rows = text_rows.transpose(3, 0, 2, 1, 4)
    full_img = lax.all_to_all(joined, "seq", 0, 0, tiled=True)
    full_txt = lax.all_to_all(text_rows, "seq", 0, 0, tiled=True)
    img_len = img_dev * seq
    head_rows, local_max = attention(text_len, full_img, full_txt)
    token_rows = lax.all_to_all(head_rows, "seq", 0, 0, tiled=True)
    weight = lax.all_gather(proj_weight, ("cfg", "req", "seq"), axis=0, tiled=True)
    projected = jnp.einsum(
        "hptd,hdo->pto",
        token_rows,
        weight.reshape(seq, HEADS // seq * HD, weight.shape[1]),
        preferred_element_type=jnp.float32,
    )
    mod_rows = modulation[0]
    hidden = img_hidden[0].astype(jnp.float32) + mod_rows[:, 0][:, None, :] * projected
    average = jnp.mean(hidden, axis=2, keepdims=True)
    centred = hidden - average
    variance = jnp.mean(centred * centred, axis=2, keepdims=True)
    normed = (
        centred / jnp.sqrt(variance + norm_eps) * (1.0 + mod_rows[:, 1][:, None, :])
        + mod_rows[:, 2][:, None, :]
    ).astype(jnp.bfloat16)
    velocity = jnp.einsum("ptd,dc->ptc", normed, final_weight, preferred_element_type=jnp.float32)
    half_chan = latents.shape[2]
    copy_pos = lax.axis_index("cfg")
    own_part = lax.dynamic_slice_in_dim(velocity, copy_pos * half_chan, half_chan, 2)
    other_part = lax.dynamic_slice_in_dim(velocity, (1 - copy_pos) * half_chan, half_chan, 2)
    partner = swapped(other_part, "cfg", 0)
    is_cond = copy_pos == 0
    cond_vel = jnp.where(is_cond, own_part, partner)
    uncond_vel = jnp.where(is_cond, partner, own_part)
    guided = uncond_vel + guidance[:, None, None] * (cond_vel - uncond_vel)
    square_sum = jnp.sum(guided * guided, axis=(1, 2))
    stats = jnp.concatenate([square_sum, local_max])
    gathered = lax.all_to_all(
        jnp.broadcast_to(stats[None], (seq, stats.shape[0])), "seq", 0, 0, tiled=True
    )
    total_sq = jnp.sum(gathered[:, :local_prompts], axis=0)
    global_max = jnp.max(gathered[:, local_prompts:], axis=0)
    vel_norm = jnp.sqrt(total_sq / (img_len * half_chan) + norm_eps)
    euler_step = sigma_of(t_index + 1) - sigma_of(t_index)
    advanced = latents + euler_step[:, None, None] * guided
    return (advanced, vel_norm.reshape(1, local_prompts), global_max.reshape(1, local_prompts))


def solution(mesh):
    return jax.shard_map(
        shards,
        mesh=mesh,
        in_specs=(
            P("cfg", "req", "seq", None),
            P("cfg", "req", "seq", None),
            P("req"),
            P("req"),
            P("req"),
            P("cfg", "req", None, None),
            P("cfg", "req", "seq", None),
            P("req", "seq", "cfg"),
            P(("cfg", "req", "seq"), None),
            P(),
        ),
        out_specs=(P("req", "seq", "cfg"), P("cfg", "req"), P("cfg", "req")),
        check_vma=False,
    )
```

```python
import functools
import math

import jax
import jax.numpy as jnp
from jax import lax
from jax.experimental import pallas as pl
from jax.experimental.pallas import tpu as pltpu
from jax.sharding import PartitionSpec as P

HEADS = 16
HD = 128
STEPS = 4
BQ = 512


time_shift = 1.15
norm_eps = 1e-06


def swapped(value, axis, stride):
    return lax.ppermute(value, axis, [(i, i ^ 1 << stride) for i in range(lax.axis_size(axis))])


def sigma_of(step_index):
    fraction = 1.0 - step_index.astype(jnp.float32) / STEPS
    lifted = fraction * math.exp(time_shift)
    return lifted / (lifted + 1.0 - fraction)


def attn_kernel(tl_ref, q_ref, kt_ref, vt_ref, ki_ref, vi_ref, o_ref, m_ref):
    p = pl.program_id(0)
    q = q_ref[...].reshape(-1, HD)
    kt = kt_ref[...].reshape(-1, HD)
    vt = vt_ref[...].reshape(-1, HD)
    ki = ki_ref[...].reshape(-1, HD)
    vi = vi_ref[...].reshape(-1, HD)
    dims = (((1,), (1,)), ((), ()))
    st = lax.dot_general(q, kt, dims, preferred_element_type=jnp.float32) * HD ** (-0.5)
    si = lax.dot_general(q, ki, dims, preferred_element_type=jnp.float32) * HD ** (-0.5)
    col = lax.broadcasted_iota(jnp.int32, st.shape, 1)
    st = jnp.where(col < tl_ref[p], st, -jnp.inf)
    m = jnp.maximum(jnp.max(st, axis=1, keepdims=True), jnp.max(si, axis=1, keepdims=True))
    et = jnp.exp(st - m)
    ei = jnp.exp(si - m)
    inv = 1.0 / (jnp.sum(et, axis=1, keepdims=True) + jnp.sum(ei, axis=1, keepdims=True))
    pt = (et * inv).astype(jnp.bfloat16)
    pi = (ei * inv).astype(jnp.bfloat16)
    o = jnp.dot(pt, vt, preferred_element_type=jnp.float32)
    o = o + jnp.dot(pi, vi, preferred_element_type=jnp.float32)
    o_ref[...] = o.astype(o_ref.dtype).reshape(o_ref.shape)
    m_ref[...] = jnp.full(m_ref.shape, jnp.max(m), jnp.float32)


def attention(text_len, img, txt):
    src, prompts, _, rows, _ = img.shape
    trows = txt.shape[3]
    img_len = src * rows
    txt_len = src * trows
    per = BQ // rows
    nq = src // per
    grid_spec = pltpu.PrefetchScalarGridSpec(
        num_scalar_prefetch=1,
        grid=(prompts, nq),
        in_specs=[
            pl.BlockSpec((per, None, None, rows, HD), lambda p, i, tl: (i, p, 0, 0, 0)),
            pl.BlockSpec((src, None, None, trows, HD), lambda p, i, tl: (0, p, 0, 0, 0)),
            pl.BlockSpec((src, None, None, trows, HD), lambda p, i, tl: (0, p, 1, 0, 0)),
            pl.BlockSpec((src, None, None, rows, HD), lambda p, i, tl: (0, p, 1, 0, 0)),
            pl.BlockSpec((src, None, None, rows, HD), lambda p, i, tl: (0, p, 2, 0, 0)),
        ],
        out_specs=[
            pl.BlockSpec((per, None, rows, HD), lambda p, i, tl: (i, p, 0, 0)),
            pl.BlockSpec((None, None, 8, 128), lambda p, i, tl: (p, i, 0, 0)),
        ],
    )
    cost = pl.CostEstimate(
        flops=4 * prompts * img_len * (img_len + txt_len) * HD,
        transcendentals=prompts * img_len * (img_len + txt_len),
        bytes_accessed=img.size * 2 + txt.size * 2 + prompts * img_len * HD * 2,
    )
    out, top = pl.pallas_call(
        attn_kernel,
        grid_spec=grid_spec,
        out_shape=[
            jax.ShapeDtypeStruct((src, prompts, rows, HD), jnp.bfloat16),
            jax.ShapeDtypeStruct((prompts, nq, 8, 128), jnp.float32),
        ],
        compiler_params=pltpu.CompilerParams(
            dimension_semantics=("arbitrary", "arbitrary"),
            vmem_limit_bytes=60 * 1024 * 1024,
        ),
        cost_estimate=cost,
    )(text_len, img, txt, txt, img, img)
    return out, jnp.max(top, axis=(1, 2, 3))


def shards(
    img_qkv,
    txt_kv,
    text_len,
    t_index,
    guidance,
    modulation,
    img_hidden,
    latents,
    proj_weight,
    final_weight,
):
    local_prompts = img_qkv.shape[1]
    img_dev = img_qkv.shape[2]
    txt_dev = txt_kv.shape[2]
    seq = lax.axis_size("seq")
    img_len = img_dev * seq
    outs = []
    maxes = []
    for p in range(local_prompts):
        joined = img_qkv[0, p].reshape(1, img_dev, 3, seq, HEADS // seq * HD)
        joined = joined.transpose(3, 0, 2, 1, 4)
        text_rows = txt_kv[0, p].reshape(1, txt_dev, 2, seq, HEADS // seq * HD)
        text_rows = text_rows.transpose(3, 0, 2, 1, 4)
        full_img = lax.all_to_all(joined, "seq", 0, 0, tiled=True)
        full_txt = lax.all_to_all(text_rows, "seq", 0, 0, tiled=True)
        head_rows, top = attention(text_len[p : p + 1], full_img, full_txt)
        outs.append(lax.all_to_all(head_rows, "seq", 0, 0, tiled=True))
        maxes.append(top)
    token_rows = jnp.concatenate(outs, axis=1)
    local_max = jnp.concatenate(maxes)
    weight = lax.all_gather(proj_weight, ("cfg", "req", "seq"), axis=0, tiled=True)
    projected = jnp.einsum(
        "hptd,hdo->pto",
        token_rows,
        weight.reshape(seq, HEADS // seq * HD, weight.shape[1]),
        preferred_element_type=jnp.float32,
    )
    mod_rows = modulation[0]
    hidden = img_hidden[0].astype(jnp.float32) + mod_rows[:, 0][:, None, :] * projected
    average = jnp.mean(hidden, axis=2, keepdims=True)
    centred = hidden - average
    variance = jnp.mean(centred * centred, axis=2, keepdims=True)
    normed = (
        centred / jnp.sqrt(variance + norm_eps) * (1.0 + mod_rows[:, 1][:, None, :])
        + mod_rows[:, 2][:, None, :]
    ).astype(jnp.bfloat16)
    velocity = jnp.einsum("ptd,dc->ptc", normed, final_weight, preferred_element_type=jnp.float32)
    half_chan = latents.shape[2]
    copy_pos = lax.axis_index("cfg")
    own_part = lax.dynamic_slice_in_dim(velocity, copy_pos * half_chan, half_chan, 2)
    other_part = lax.dynamic_slice_in_dim(velocity, (1 - copy_pos) * half_chan, half_chan, 2)
    partner = swapped(other_part, "cfg", 0)
    is_cond = copy_pos == 0
    cond_vel = jnp.where(is_cond, own_part, partner)
    uncond_vel = jnp.where(is_cond, partner, own_part)
    guided = uncond_vel + guidance[:, None, None] * (cond_vel - uncond_vel)
    square_sum = jnp.sum(guided * guided, axis=(1, 2))
    stats = jnp.concatenate([square_sum, local_max])
    gathered = lax.all_to_all(
        jnp.broadcast_to(stats[None], (seq, stats.shape[0])), "seq", 0, 0, tiled=True
    )
    total_sq = jnp.sum(gathered[:, :local_prompts], axis=0)
    global_max = jnp.max(gathered[:, local_prompts:], axis=0)
    vel_norm = jnp.sqrt(total_sq / (img_len * half_chan) + norm_eps)
    euler_step = sigma_of(t_index + 1) - sigma_of(t_index)
    advanced = latents + euler_step[:, None, None] * guided
    return (advanced, vel_norm.reshape(1, local_prompts), global_max.reshape(1, local_prompts))


def solution(mesh):
    return jax.shard_map(
        shards,
        mesh=mesh,
        in_specs=(
            P("cfg", "req", "seq", None),
            P("cfg", "req", "seq", None),
            P("req"),
            P("req"),
            P("req"),
            P("cfg", "req", None, None),
            P("cfg", "req", "seq", None),
            P("req", "seq", "cfg"),
            P(("cfg", "req", "seq"), None),
            P(),
        ),
        out_specs=(P("req", "seq", "cfg"), P("cfg", "req"), P("cfg", "req")),
        check_vma=False,
    )
```

```python
import functools
import math

import jax
import jax.numpy as jnp
from jax import lax
from jax.experimental import pallas as pl
from jax.experimental.pallas import tpu as pltpu
from jax.sharding import PartitionSpec as P

HEADS = 16
HD = 128
STEPS = 4
BQ = 256


time_shift = 1.15
norm_eps = 1e-06


def swapped(value, axis, stride):
    return lax.ppermute(value, axis, [(i, i ^ 1 << stride) for i in range(lax.axis_size(axis))])


def sigma_of(step_index):
    fraction = 1.0 - step_index.astype(jnp.float32) / STEPS
    lifted = fraction * math.exp(time_shift)
    return lifted / (lifted + 1.0 - fraction)


def attn_kernel(tl_ref, q_ref, kt_ref, vt_ref, ki_ref, vi_ref, o_ref, m_ref):
    p = pl.program_id(0)
    q = q_ref[...].reshape(-1, HD)
    kt = kt_ref[...].reshape(-1, HD)
    vt = vt_ref[...].reshape(-1, HD)
    ki = ki_ref[...].reshape(-1, HD)
    vi = vi_ref[...].reshape(-1, HD)
    dims = (((1,), (1,)), ((), ()))
    st = lax.dot_general(q, kt, dims, preferred_element_type=jnp.float32) * HD ** (-0.5)
    si = lax.dot_general(q, ki, dims, preferred_element_type=jnp.float32) * HD ** (-0.5)
    col = lax.broadcasted_iota(jnp.int32, st.shape, 1)
    st = jnp.where(col < tl_ref[p], st, -jnp.inf)
    m = jnp.maximum(jnp.max(st, axis=1, keepdims=True), jnp.max(si, axis=1, keepdims=True))
    et = jnp.exp(st - m)
    ei = jnp.exp(si - m)
    inv = 1.0 / (jnp.sum(et, axis=1, keepdims=True) + jnp.sum(ei, axis=1, keepdims=True))
    pt = (et * inv).astype(jnp.bfloat16)
    pi = (ei * inv).astype(jnp.bfloat16)
    o = jnp.dot(pt, vt, preferred_element_type=jnp.float32)
    o = o + jnp.dot(pi, vi, preferred_element_type=jnp.float32)
    o_ref[...] = o.astype(o_ref.dtype).reshape(o_ref.shape)
    m_ref[...] = jnp.full(m_ref.shape, jnp.max(m), jnp.float32)


def attention(text_len, img, txt):
    src, prompts, _, rows, _ = img.shape
    trows = txt.shape[3]
    img_len = src * rows
    txt_len = src * trows
    per = BQ // rows
    nq = src // per
    grid_spec = pltpu.PrefetchScalarGridSpec(
        num_scalar_prefetch=1,
        grid=(prompts, nq),
        in_specs=[
            pl.BlockSpec((per, None, None, rows, HD), lambda p, i, tl: (i, p, 0, 0, 0)),
            pl.BlockSpec((src, None, None, trows, HD), lambda p, i, tl: (0, p, 0, 0, 0)),
            pl.BlockSpec((src, None, None, trows, HD), lambda p, i, tl: (0, p, 1, 0, 0)),
            pl.BlockSpec((src, None, None, rows, HD), lambda p, i, tl: (0, p, 1, 0, 0)),
            pl.BlockSpec((src, None, None, rows, HD), lambda p, i, tl: (0, p, 2, 0, 0)),
        ],
        out_specs=[
            pl.BlockSpec((per, None, rows, HD), lambda p, i, tl: (i, p, 0, 0)),
            pl.BlockSpec((None, None, 8, 128), lambda p, i, tl: (p, i, 0, 0)),
        ],
    )
    cost = pl.CostEstimate(
        flops=4 * prompts * img_len * (img_len + txt_len) * HD,
        transcendentals=prompts * img_len * (img_len + txt_len),
        bytes_accessed=img.size * 2 + txt.size * 2 + prompts * img_len * HD * 2,
    )
    out, top = pl.pallas_call(
        attn_kernel,
        grid_spec=grid_spec,
        out_shape=[
            jax.ShapeDtypeStruct((src, prompts, rows, HD), jnp.bfloat16),
            jax.ShapeDtypeStruct((prompts, nq, 8, 128), jnp.float32),
        ],
        compiler_params=pltpu.CompilerParams(
            dimension_semantics=("arbitrary", "arbitrary"),
            vmem_limit_bytes=60 * 1024 * 1024,
        ),
        cost_estimate=cost,
    )(text_len, img, txt, txt, img, img)
    return out, jnp.max(top, axis=(1, 2, 3))


def shards(
    img_qkv,
    txt_kv,
    text_len,
    t_index,
    guidance,
    modulation,
    img_hidden,
    latents,
    proj_weight,
    final_weight,
):
    local_prompts = img_qkv.shape[1]
    img_dev = img_qkv.shape[2]
    txt_dev = txt_kv.shape[2]
    seq = lax.axis_size("seq")
    img_len = img_dev * seq
    outs = []
    maxes = []
    for p in range(local_prompts):
        joined = img_qkv[0, p].reshape(1, img_dev, 3, seq, HEADS // seq * HD)
        joined = joined.transpose(3, 0, 2, 1, 4)
        text_rows = txt_kv[0, p].reshape(1, txt_dev, 2, seq, HEADS // seq * HD)
        text_rows = text_rows.transpose(3, 0, 2, 1, 4)
        full_img = lax.all_to_all(joined, "seq", 0, 0, tiled=True)
        full_txt = lax.all_to_all(text_rows, "seq", 0, 0, tiled=True)
        head_rows, top = attention(text_len[p : p + 1], full_img, full_txt)
        outs.append(lax.all_to_all(head_rows, "seq", 0, 0, tiled=True))
        maxes.append(top)
    token_rows = jnp.concatenate(outs, axis=1)
    local_max = jnp.concatenate(maxes)
    weight = lax.all_gather(proj_weight, ("cfg", "req", "seq"), axis=0, tiled=True)
    projected = jnp.einsum(
        "hptd,hdo->pto",
        token_rows,
        weight.reshape(seq, HEADS // seq * HD, weight.shape[1]),
        preferred_element_type=jnp.float32,
    )
    mod_rows = modulation[0]
    hidden = img_hidden[0].astype(jnp.float32) + mod_rows[:, 0][:, None, :] * projected
    average = jnp.mean(hidden, axis=2, keepdims=True)
    centred = hidden - average
    variance = jnp.mean(centred * centred, axis=2, keepdims=True)
    normed = (
        centred / jnp.sqrt(variance + norm_eps) * (1.0 + mod_rows[:, 1][:, None, :])
        + mod_rows[:, 2][:, None, :]
    ).astype(jnp.bfloat16)
    velocity = jnp.einsum("ptd,dc->ptc", normed, final_weight, preferred_element_type=jnp.float32)
    half_chan = latents.shape[2]
    copy_pos = lax.axis_index("cfg")
    own_part = lax.dynamic_slice_in_dim(velocity, copy_pos * half_chan, half_chan, 2)
    other_part = lax.dynamic_slice_in_dim(velocity, (1 - copy_pos) * half_chan, half_chan, 2)
    partner = swapped(other_part, "cfg", 0)
    is_cond = copy_pos == 0
    cond_vel = jnp.where(is_cond, own_part, partner)
    uncond_vel = jnp.where(is_cond, partner, own_part)
    guided = uncond_vel + guidance[:, None, None] * (cond_vel - uncond_vel)
    square_sum = jnp.sum(guided * guided, axis=(1, 2))
    stats = jnp.concatenate([square_sum, local_max])
    gathered = lax.all_to_all(
        jnp.broadcast_to(stats[None], (seq, stats.shape[0])), "seq", 0, 0, tiled=True
    )
    total_sq = jnp.sum(gathered[:, :local_prompts], axis=0)
    global_max = jnp.max(gathered[:, local_prompts:], axis=0)
    vel_norm = jnp.sqrt(total_sq / (img_len * half_chan) + norm_eps)
    euler_step = sigma_of(t_index + 1) - sigma_of(t_index)
    advanced = latents + euler_step[:, None, None] * guided
    return (advanced, vel_norm.reshape(1, local_prompts), global_max.reshape(1, local_prompts))


def solution(mesh):
    return jax.shard_map(
        shards,
        mesh=mesh,
        in_specs=(
            P("cfg", "req", "seq", None),
            P("cfg", "req", "seq", None),
            P("req"),
            P("req"),
            P("req"),
            P("cfg", "req", None, None),
            P("cfg", "req", "seq", None),
            P("req", "seq", "cfg"),
            P(("cfg", "req", "seq"), None),
            P(),
        ),
        out_specs=(P("req", "seq", "cfg"), P("cfg", "req"), P("cfg", "req")),
        check_vma=False,
    )
```

```python
import functools
import math

import jax
import jax.numpy as jnp
from jax import lax
from jax.experimental import pallas as pl
from jax.experimental.pallas import tpu as pltpu
from jax.sharding import PartitionSpec as P

HEADS = 16
HD = 128
STEPS = 4
BQ = 1024
CK = 512


time_shift = 1.15
norm_eps = 1e-06


def swapped(value, axis, stride):
    return lax.ppermute(value, axis, [(i, i ^ 1 << stride) for i in range(lax.axis_size(axis))])


def sigma_of(step_index):
    fraction = 1.0 - step_index.astype(jnp.float32) / STEPS
    lifted = fraction * math.exp(time_shift)
    return lifted / (lifted + 1.0 - fraction)


def attn_kernel(tl_ref, q_ref, kt_ref, vt_ref, ki_ref, vi_ref, o_ref, m_ref):
    p = pl.program_id(0)
    dims = (((1,), (1,)), ((), ()))
    q = q_ref[...].reshape(-1, HD)
    st = lax.dot_general(q, kt_ref[...].reshape(-1, HD), dims, preferred_element_type=jnp.float32)
    st = st * HD ** (-0.5)
    col = lax.broadcasted_iota(jnp.int32, st.shape, 1)
    st = jnp.where(col < tl_ref[p], st, -jnp.inf)
    m = jnp.max(st, axis=1, keepdims=True)
    e = jnp.exp(st - m)
    l = jnp.sum(e, axis=1, keepdims=True)
    acc = jnp.dot(
        e.astype(jnp.bfloat16), vt_ref[...].reshape(-1, HD), preferred_element_type=jnp.float32
    )
    per = CK // ki_ref.shape[1]
    for c in range(ki_ref.shape[0] // per):
        k = ki_ref[c * per : (c + 1) * per].reshape(-1, HD)
        v = vi_ref[c * per : (c + 1) * per].reshape(-1, HD)
        s = lax.dot_general(q, k, dims, preferred_element_type=jnp.float32) * HD ** (-0.5)
        m_new = jnp.maximum(m, jnp.max(s, axis=1, keepdims=True))
        alpha = jnp.exp(m - m_new)
        e = jnp.exp(s - m_new)
        l = alpha * l + jnp.sum(e, axis=1, keepdims=True)
        acc = alpha * acc + jnp.dot(e.astype(jnp.bfloat16), v, preferred_element_type=jnp.float32)
        m = m_new
    o = acc * (1.0 / l)
    o_ref[...] = o.astype(o_ref.dtype).reshape(o_ref.shape)
    m_ref[...] = jnp.full(m_ref.shape, jnp.max(m), jnp.float32)


def attention(text_len, img, txt):
    src, prompts, _, rows, _ = img.shape
    trows = txt.shape[3]
    img_len = src * rows
    txt_len = src * trows
    per = BQ // rows
    nq = src // per
    grid_spec = pltpu.PrefetchScalarGridSpec(
        num_scalar_prefetch=1,
        grid=(prompts, nq),
        in_specs=[
            pl.BlockSpec((per, None, None, rows, HD), lambda p, i, tl: (i, p, 0, 0, 0)),
            pl.BlockSpec((src, None, None, trows, HD), lambda p, i, tl: (0, p, 0, 0, 0)),
            pl.BlockSpec((src, None, None, trows, HD), lambda p, i, tl: (0, p, 1, 0, 0)),
            pl.BlockSpec((src, None, None, rows, HD), lambda p, i, tl: (0, p, 1, 0, 0)),
            pl.BlockSpec((src, None, None, rows, HD), lambda p, i, tl: (0, p, 2, 0, 0)),
        ],
        out_specs=[
            pl.BlockSpec((per, None, rows, HD), lambda p, i, tl: (i, p, 0, 0)),
            pl.BlockSpec((None, None, 8, 128), lambda p, i, tl: (p, i, 0, 0)),
        ],
    )
    cost = pl.CostEstimate(
        flops=4 * prompts * img_len * (img_len + txt_len) * HD,
        transcendentals=prompts * img_len * (img_len + txt_len),
        bytes_accessed=img.size * 2 + txt.size * 2 + prompts * img_len * HD * 2,
    )
    out, top = pl.pallas_call(
        attn_kernel,
        grid_spec=grid_spec,
        out_shape=[
            jax.ShapeDtypeStruct((src, prompts, rows, HD), jnp.bfloat16),
            jax.ShapeDtypeStruct((prompts, nq, 8, 128), jnp.float32),
        ],
        compiler_params=pltpu.CompilerParams(
            dimension_semantics=("arbitrary", "arbitrary"),
            vmem_limit_bytes=60 * 1024 * 1024,
        ),
        cost_estimate=cost,
    )(text_len, img, txt, txt, img, img)
    return out, jnp.max(top, axis=(1, 2, 3))


def shards(
    img_qkv,
    txt_kv,
    text_len,
    t_index,
    guidance,
    modulation,
    img_hidden,
    latents,
    proj_weight,
    final_weight,
):
    local_prompts = img_qkv.shape[1]
    img_dev = img_qkv.shape[2]
    txt_dev = txt_kv.shape[2]
    seq = lax.axis_size("seq")
    img_len = img_dev * seq
    outs = []
    maxes = []
    for p in range(local_prompts):
        joined = img_qkv[0, p].reshape(1, img_dev, 3, seq, HEADS // seq * HD)
        joined = joined.transpose(3, 0, 2, 1, 4)
        text_rows = txt_kv[0, p].reshape(1, txt_dev, 2, seq, HEADS // seq * HD)
        text_rows = text_rows.transpose(3, 0, 2, 1, 4)
        full_img = lax.all_to_all(joined, "seq", 0, 0, tiled=True)
        full_txt = lax.all_to_all(text_rows, "seq", 0, 0, tiled=True)
        head_rows, top = attention(text_len[p : p + 1], full_img, full_txt)
        outs.append(lax.all_to_all(head_rows, "seq", 0, 0, tiled=True))
        maxes.append(top)
    token_rows = jnp.concatenate(outs, axis=1)
    local_max = jnp.concatenate(maxes)
    weight = lax.all_gather(proj_weight, ("cfg", "req", "seq"), axis=0, tiled=True)
    projected = jnp.einsum(
        "hptd,hdo->pto",
        token_rows,
        weight.reshape(seq, HEADS // seq * HD, weight.shape[1]),
        preferred_element_type=jnp.float32,
    )
    mod_rows = modulation[0]
    hidden = img_hidden[0].astype(jnp.float32) + mod_rows[:, 0][:, None, :] * projected
    average = jnp.mean(hidden, axis=2, keepdims=True)
    centred = hidden - average
    variance = jnp.mean(centred * centred, axis=2, keepdims=True)
    normed = (
        centred / jnp.sqrt(variance + norm_eps) * (1.0 + mod_rows[:, 1][:, None, :])
        + mod_rows[:, 2][:, None, :]
    ).astype(jnp.bfloat16)
    velocity = jnp.einsum("ptd,dc->ptc", normed, final_weight, preferred_element_type=jnp.float32)
    half_chan = latents.shape[2]
    copy_pos = lax.axis_index("cfg")
    own_part = lax.dynamic_slice_in_dim(velocity, copy_pos * half_chan, half_chan, 2)
    other_part = lax.dynamic_slice_in_dim(velocity, (1 - copy_pos) * half_chan, half_chan, 2)
    partner = swapped(other_part, "cfg", 0)
    is_cond = copy_pos == 0
    cond_vel = jnp.where(is_cond, own_part, partner)
    uncond_vel = jnp.where(is_cond, partner, own_part)
    guided = uncond_vel + guidance[:, None, None] * (cond_vel - uncond_vel)
    square_sum = jnp.sum(guided * guided, axis=(1, 2))
    stats = jnp.concatenate([square_sum, local_max])
    gathered = lax.all_to_all(
        jnp.broadcast_to(stats[None], (seq, stats.shape[0])), "seq", 0, 0, tiled=True
    )
    total_sq = jnp.sum(gathered[:, :local_prompts], axis=0)
    global_max = jnp.max(gathered[:, local_prompts:], axis=0)
    vel_norm = jnp.sqrt(total_sq / (img_len * half_chan) + norm_eps)
    euler_step = sigma_of(t_index + 1) - sigma_of(t_index)
    advanced = latents + euler_step[:, None, None] * guided
    return (advanced, vel_norm.reshape(1, local_prompts), global_max.reshape(1, local_prompts))


def solution(mesh):
    return jax.shard_map(
        shards,
        mesh=mesh,
        in_specs=(
            P("cfg", "req", "seq", None),
            P("cfg", "req", "seq", None),
            P("req"),
            P("req"),
            P("req"),
            P("cfg", "req", None, None),
            P("cfg", "req", "seq", None),
            P("req", "seq", "cfg"),
            P(("cfg", "req", "seq"), None),
            P(),
        ),
        out_specs=(P("req", "seq", "cfg"), P("cfg", "req"), P("cfg", "req")),
        check_vma=False,
    )
```

```python
import functools
import math

import jax
import jax.numpy as jnp
from jax import lax
from jax.experimental import pallas as pl
from jax.experimental.pallas import tpu as pltpu
from jax.sharding import PartitionSpec as P

HEADS = 16
HD = 128
STEPS = 4
BQ = 1024
CK = 512


time_shift = 1.15
norm_eps = 1e-06


def swapped(value, axis, stride):
    return lax.ppermute(value, axis, [(i, i ^ 1 << stride) for i in range(lax.axis_size(axis))])


def sigma_of(step_index):
    fraction = 1.0 - step_index.astype(jnp.float32) / STEPS
    lifted = fraction * math.exp(time_shift)
    return lifted / (lifted + 1.0 - fraction)


def attn_kernel(tl_ref, q_ref, kt_ref, vt_ref, ki_ref, vi_ref, o_ref, m_ref):
    dims = (((1,), (1,)), ((), ()))
    q = q_ref[...].reshape(-1, HD)
    st = lax.dot_general(q, kt_ref[...].reshape(-1, HD), dims, preferred_element_type=jnp.float32)
    st = st * HD ** (-0.5)
    col = lax.broadcasted_iota(jnp.int32, st.shape, 1)
    st = jnp.where(col < tl_ref[0], st, -jnp.inf)
    m = jnp.max(st, axis=1, keepdims=True)
    e = jnp.exp(st - m)
    l = jnp.sum(e, axis=1, keepdims=True)
    acc = jnp.dot(
        e.astype(jnp.bfloat16), vt_ref[...].reshape(-1, HD), preferred_element_type=jnp.float32
    )
    per = CK // ki_ref.shape[1]
    for c in range(ki_ref.shape[0] // per):
        k = ki_ref[c * per : (c + 1) * per].reshape(-1, HD)
        v = vi_ref[c * per : (c + 1) * per].reshape(-1, HD)
        s = lax.dot_general(q, k, dims, preferred_element_type=jnp.float32) * HD ** (-0.5)
        m_new = jnp.maximum(m, jnp.max(s, axis=1, keepdims=True))
        alpha = jnp.exp(m - m_new)
        e = jnp.exp(s - m_new)
        l = alpha * l + jnp.sum(e, axis=1, keepdims=True)
        acc = alpha * acc + jnp.dot(e.astype(jnp.bfloat16), v, preferred_element_type=jnp.float32)
        m = m_new
    o = acc * (1.0 / l)
    o_ref[...] = o.astype(o_ref.dtype).reshape(o_ref.shape)
    m_ref[...] = jnp.full(m_ref.shape, jnp.max(m), jnp.float32)


def attention(text_len, buf, rows, trows):
    src = buf.shape[0]
    img_len = src * rows
    txt_len = src * trows
    per = BQ // rows
    nq = src // per
    grid_spec = pltpu.PrefetchScalarGridSpec(
        num_scalar_prefetch=1,
        grid=(1, nq),
        in_specs=[
            pl.BlockSpec((per, rows, HD), lambda p, i, tl: (i, 0, 0)),
            pl.BlockSpec((src, trows, HD), lambda p, i, tl: (0, 3 * rows // trows, 0)),
            pl.BlockSpec((src, trows, HD), lambda p, i, tl: (0, 3 * rows // trows + 1, 0)),
            pl.BlockSpec((src, rows, HD), lambda p, i, tl: (0, 1, 0)),
            pl.BlockSpec((src, rows, HD), lambda p, i, tl: (0, 2, 0)),
        ],
        out_specs=[
            pl.BlockSpec((per, rows, HD), lambda p, i, tl: (i, 0, 0)),
            pl.BlockSpec((None, 8, 128), lambda p, i, tl: (i, 0, 0)),
        ],
    )
    cost = pl.CostEstimate(
        flops=4 * img_len * (img_len + txt_len) * HD,
        transcendentals=img_len * (img_len + txt_len),
        bytes_accessed=buf.size * 2 + img_len * HD * 2,
    )
    out, top = pl.pallas_call(
        attn_kernel,
        grid_spec=grid_spec,
        out_shape=[
            jax.ShapeDtypeStruct((src, rows, HD), jnp.bfloat16),
            jax.ShapeDtypeStruct((nq, 8, 128), jnp.float32),
        ],
        compiler_params=pltpu.CompilerParams(
            dimension_semantics=("arbitrary", "arbitrary"),
            vmem_limit_bytes=60 * 1024 * 1024,
        ),
        cost_estimate=cost,
    )(text_len, buf, buf, buf, buf, buf)
    return out, jnp.max(top)[None]


def shards(
    img_qkv,
    txt_kv,
    text_len,
    t_index,
    guidance,
    modulation,
    img_hidden,
    latents,
    proj_weight,
    final_weight,
):
    local_prompts = img_qkv.shape[1]
    img_dev = img_qkv.shape[2]
    txt_dev = txt_kv.shape[2]
    seq = lax.axis_size("seq")
    img_len = img_dev * seq
    outs = []
    maxes = []
    for p in range(local_prompts):
        joined = img_qkv[0, p].reshape(img_dev, 3, seq, HEADS // seq * HD)
        joined = joined.transpose(2, 1, 0, 3).reshape(seq, 3 * img_dev, HD)
        text_rows = txt_kv[0, p].reshape(txt_dev, 2, seq, HEADS // seq * HD)
        text_rows = text_rows.transpose(2, 1, 0, 3).reshape(seq, 2 * txt_dev, HD)
        buf = lax.all_to_all(
            jnp.concatenate([joined, text_rows], axis=1), "seq", 0, 0, tiled=True
        )
        head_rows, top = attention(text_len[p : p + 1], buf, img_dev, txt_dev)
        outs.append(lax.all_to_all(head_rows, "seq", 0, 0, tiled=True)[:, None])
        maxes.append(top)
    token_rows = jnp.concatenate(outs, axis=1)
    local_max = jnp.concatenate(maxes)
    weight = lax.all_gather(proj_weight, ("cfg", "req", "seq"), axis=0, tiled=True)
    projected = jnp.einsum(
        "hptd,hdo->pto",
        token_rows,
        weight.reshape(seq, HEADS // seq * HD, weight.shape[1]),
        preferred_element_type=jnp.float32,
    )
    mod_rows = modulation[0]
    hidden = img_hidden[0].astype(jnp.float32) + mod_rows[:, 0][:, None, :] * projected
    average = jnp.mean(hidden, axis=2, keepdims=True)
    centred = hidden - average
    variance = jnp.mean(centred * centred, axis=2, keepdims=True)
    normed = (
        centred / jnp.sqrt(variance + norm_eps) * (1.0 + mod_rows[:, 1][:, None, :])
        + mod_rows[:, 2][:, None, :]
    ).astype(jnp.bfloat16)
    velocity = jnp.einsum("ptd,dc->ptc", normed, final_weight, preferred_element_type=jnp.float32)
    half_chan = latents.shape[2]
    copy_pos = lax.axis_index("cfg")
    own_part = lax.dynamic_slice_in_dim(velocity, copy_pos * half_chan, half_chan, 2)
    other_part = lax.dynamic_slice_in_dim(velocity, (1 - copy_pos) * half_chan, half_chan, 2)
    partner = swapped(other_part, "cfg", 0)
    is_cond = copy_pos == 0
    cond_vel = jnp.where(is_cond, own_part, partner)
    uncond_vel = jnp.where(is_cond, partner, own_part)
    guided = uncond_vel + guidance[:, None, None] * (cond_vel - uncond_vel)
    square_sum = jnp.sum(guided * guided, axis=(1, 2))
    stats = jnp.concatenate([square_sum, local_max])
    gathered = lax.all_to_all(
        jnp.broadcast_to(stats[None], (seq, stats.shape[0])), "seq", 0, 0, tiled=True
    )
    total_sq = jnp.sum(gathered[:, :local_prompts], axis=0)
    global_max = jnp.max(gathered[:, local_prompts:], axis=0)
    vel_norm = jnp.sqrt(total_sq / (img_len * half_chan) + norm_eps)
    euler_step = sigma_of(t_index + 1) - sigma_of(t_index)
    advanced = latents + euler_step[:, None, None] * guided
    return (advanced, vel_norm.reshape(1, local_prompts), global_max.reshape(1, local_prompts))


def solution(mesh):
    return jax.shard_map(
        shards,
        mesh=mesh,
        in_specs=(
            P("cfg", "req", "seq", None),
            P("cfg", "req", "seq", None),
            P("req"),
            P("req"),
            P("req"),
            P("cfg", "req", None, None),
            P("cfg", "req", "seq", None),
            P("req", "seq", "cfg"),
            P(("cfg", "req", "seq"), None),
            P(),
        ),
        out_specs=(P("req", "seq", "cfg"), P("cfg", "req"), P("cfg", "req")),
        check_vma=False,
    )
```

```python
import functools
import math

import jax
import jax.numpy as jnp
from jax import lax
from jax.experimental import pallas as pl
from jax.experimental.pallas import tpu as pltpu
from jax.sharding import PartitionSpec as P

HEADS = 16
HD = 128
STEPS = 4
BQ = 1024
CK = 512


time_shift = 1.15
norm_eps = 1e-06


def swapped(value, axis, stride):
    return lax.ppermute(value, axis, [(i, i ^ 1 << stride) for i in range(lax.axis_size(axis))])


def sigma_of(step_index):
    fraction = 1.0 - step_index.astype(jnp.float32) / STEPS
    lifted = fraction * math.exp(time_shift)
    return lifted / (lifted + 1.0 - fraction)


def attn_kernel(tl_ref, q_ref, kt_ref, vt_ref, ki_ref, vi_ref, o_ref, m_ref):
    dims = (((1,), (1,)), ((), ()))
    q = q_ref[...].reshape(-1, HD)
    st = lax.dot_general(q, kt_ref[...].reshape(-1, HD), dims, preferred_element_type=jnp.float32)
    st = st * HD ** (-0.5)
    col = lax.broadcasted_iota(jnp.int32, st.shape, 1)
    st = jnp.where(col < tl_ref[0], st, -jnp.inf)
    m = jnp.max(st, axis=1, keepdims=True)
    e = jnp.exp(st - m)
    l = jnp.sum(e, axis=1, keepdims=True)
    acc = jnp.dot(
        e.astype(jnp.bfloat16), vt_ref[...].reshape(-1, HD), preferred_element_type=jnp.float32
    )
    per = CK // ki_ref.shape[1]
    for c in range(ki_ref.shape[0] // per):
        k = ki_ref[c * per : (c + 1) * per].reshape(-1, HD)
        v = vi_ref[c * per : (c + 1) * per].reshape(-1, HD)
        s = lax.dot_general(q, k, dims, preferred_element_type=jnp.float32) * HD ** (-0.5)
        m_new = jnp.maximum(m, jnp.max(s, axis=1, keepdims=True))
        alpha = jnp.exp(m - m_new)
        e = jnp.exp(s - m_new)
        l = alpha * l + jnp.sum(e, axis=1, keepdims=True)
        acc = alpha * acc + jnp.dot(e.astype(jnp.bfloat16), v, preferred_element_type=jnp.float32)
        m = m_new
    o = acc * (1.0 / l)
    o_ref[...] = o.astype(o_ref.dtype).reshape(o_ref.shape)
    m_ref[...] = jnp.full(m_ref.shape, jnp.max(m), jnp.float32)


def attention(text_len, buf, rows, trows):
    src = buf.shape[0]
    img_len = src * rows
    txt_len = src * trows
    per = BQ // rows
    nq = src // per
    grid_spec = pltpu.PrefetchScalarGridSpec(
        num_scalar_prefetch=1,
        grid=(1, nq),
        in_specs=[
            pl.BlockSpec((per, rows, HD), lambda p, i, tl: (i, 0, 0)),
            pl.BlockSpec((src, trows, HD), lambda p, i, tl: (0, 3 * rows // trows, 0)),
            pl.BlockSpec((src, trows, HD), lambda p, i, tl: (0, 3 * rows // trows + 1, 0)),
            pl.BlockSpec((src, rows, HD), lambda p, i, tl: (0, 1, 0)),
            pl.BlockSpec((src, rows, HD), lambda p, i, tl: (0, 2, 0)),
        ],
        out_specs=[
            pl.BlockSpec((per, rows, HD), lambda p, i, tl: (i, 0, 0)),
            pl.BlockSpec((None, 8, 128), lambda p, i, tl: (i, 0, 0)),
        ],
    )
    cost = pl.CostEstimate(
        flops=4 * img_len * (img_len + txt_len) * HD,
        transcendentals=img_len * (img_len + txt_len),
        bytes_accessed=buf.size * 2 + img_len * HD * 2,
    )
    out, top = pl.pallas_call(
        attn_kernel,
        grid_spec=grid_spec,
        out_shape=[
            jax.ShapeDtypeStruct((src, rows, HD), jnp.bfloat16),
            jax.ShapeDtypeStruct((nq, 8, 128), jnp.float32),
        ],
        compiler_params=pltpu.CompilerParams(
            dimension_semantics=("arbitrary", "arbitrary"),
            vmem_limit_bytes=60 * 1024 * 1024,
        ),
        cost_estimate=cost,
    )(text_len, buf, buf, buf, buf, buf)
    return out, jnp.max(top)[None]


def shards(
    img_qkv,
    txt_kv,
    text_len,
    t_index,
    guidance,
    modulation,
    img_hidden,
    latents,
    proj_weight,
    final_weight,
):
    local_prompts = img_qkv.shape[1]
    img_dev = img_qkv.shape[2]
    txt_dev = txt_kv.shape[2]
    seq = lax.axis_size("seq")
    img_len = img_dev * seq
    outs = []
    maxes = []
    for p in range(local_prompts):
        joined = img_qkv[0, p].reshape(img_dev, 3, seq, HEADS // seq * HD)
        joined = joined.transpose(2, 1, 0, 3).reshape(seq, 3 * img_dev, HD)
        text_rows = txt_kv[0, p].reshape(txt_dev, 2, seq, HEADS // seq * HD)
        text_rows = text_rows.transpose(2, 1, 0, 3).reshape(seq, 2 * txt_dev, HD)
        buf = lax.all_to_all(
            jnp.concatenate([joined, text_rows], axis=1), "seq", 0, 0, tiled=True
        )
        head_rows, top = attention(text_len[p : p + 1], buf, img_dev, txt_dev)
        outs.append(lax.all_to_all(head_rows, "seq", 0, 0, tiled=True)[:, None])
        maxes.append(top)
    token_rows = jnp.concatenate(outs, axis=1)
    local_max = jnp.concatenate(maxes)
    weight_half = lax.all_gather(proj_weight, ("req", "seq"), axis=0, tiled=True)
    other_half = swapped(weight_half, "cfg", 0)
    first = lax.axis_index("cfg") == 0
    weight = jnp.concatenate(
        [jnp.where(first, weight_half, other_half), jnp.where(first, other_half, weight_half)], axis=0
    )
    projected = jnp.einsum(
        "hptd,hdo->pto",
        token_rows,
        weight.reshape(seq, HEADS // seq * HD, weight.shape[1]),
        preferred_element_type=jnp.float32,
    )
    mod_rows = modulation[0]
    hidden = img_hidden[0].astype(jnp.float32) + mod_rows[:, 0][:, None, :] * projected
    average = jnp.mean(hidden, axis=2, keepdims=True)
    centred = hidden - average
    variance = jnp.mean(centred * centred, axis=2, keepdims=True)
    normed = (
        centred / jnp.sqrt(variance + norm_eps) * (1.0 + mod_rows[:, 1][:, None, :])
        + mod_rows[:, 2][:, None, :]
    ).astype(jnp.bfloat16)
    velocity = jnp.einsum("ptd,dc->ptc", normed, final_weight, preferred_element_type=jnp.float32)
    half_chan = latents.shape[2]
    copy_pos = lax.axis_index("cfg")
    own_part = lax.dynamic_slice_in_dim(velocity, copy_pos * half_chan, half_chan, 2)
    other_part = lax.dynamic_slice_in_dim(velocity, (1 - copy_pos) * half_chan, half_chan, 2)
    partner = swapped(other_part, "cfg", 0)
    is_cond = copy_pos == 0
    cond_vel = jnp.where(is_cond, own_part, partner)
    uncond_vel = jnp.where(is_cond, partner, own_part)
    guided = uncond_vel + guidance[:, None, None] * (cond_vel - uncond_vel)
    square_sum = jnp.sum(guided * guided, axis=(1, 2))
    stats = jnp.concatenate([square_sum, local_max])
    gathered = lax.all_to_all(
        jnp.broadcast_to(stats[None], (seq, stats.shape[0])), "seq", 0, 0, tiled=True
    )
    total_sq = jnp.sum(gathered[:, :local_prompts], axis=0)
    global_max = jnp.max(gathered[:, local_prompts:], axis=0)
    vel_norm = jnp.sqrt(total_sq / (img_len * half_chan) + norm_eps)
    euler_step = sigma_of(t_index + 1) - sigma_of(t_index)
    advanced = latents + euler_step[:, None, None] * guided
    return (advanced, vel_norm.reshape(1, local_prompts), global_max.reshape(1, local_prompts))


def solution(mesh):
    return jax.shard_map(
        shards,
        mesh=mesh,
        in_specs=(
            P("cfg", "req", "seq", None),
            P("cfg", "req", "seq", None),
            P("req"),
            P("req"),
            P("req"),
            P("cfg", "req", None, None),
            P("cfg", "req", "seq", None),
            P("req", "seq", "cfg"),
            P(("cfg", "req", "seq"), None),
            P(),
        ),
        out_specs=(P("req", "seq", "cfg"), P("cfg", "req"), P("cfg", "req")),
        check_vma=False,
    )
```

```python
import functools
import math

import jax
import jax.numpy as jnp
from jax import lax
from jax.experimental import pallas as pl
from jax.experimental.pallas import tpu as pltpu
from jax.sharding import PartitionSpec as P

HEADS = 16
HD = 128
STEPS = 4
BQ = 1024
CK = 512


time_shift = 1.15
norm_eps = 1e-06


def swapped(value, axis, stride):
    return lax.ppermute(value, axis, [(i, i ^ 1 << stride) for i in range(lax.axis_size(axis))])


def sigma_of(step_index):
    fraction = 1.0 - step_index.astype(jnp.float32) / STEPS
    lifted = fraction * math.exp(time_shift)
    return lifted / (lifted + 1.0 - fraction)


def attn_kernel(tl_ref, q_ref, kt_ref, vt_ref, ki_ref, vi_ref, o_ref, m_ref):
    dims = (((1,), (1,)), ((), ()))
    q = q_ref[...].reshape(-1, HD)
    st = lax.dot_general(q, kt_ref[...].reshape(-1, HD), dims, preferred_element_type=jnp.float32)
    st = st * HD ** (-0.5)
    col = lax.broadcasted_iota(jnp.int32, st.shape, 1)
    st = jnp.where(col < tl_ref[0], st, -jnp.inf)
    m = jnp.max(st, axis=1, keepdims=True)
    e = jnp.exp(st - m)
    l = jnp.sum(e, axis=1, keepdims=True)
    acc = jnp.dot(
        e.astype(jnp.bfloat16), vt_ref[...].reshape(-1, HD), preferred_element_type=jnp.float32
    )
    per = CK // ki_ref.shape[1]
    for c in range(ki_ref.shape[0] // per):
        k = ki_ref[c * per : (c + 1) * per].reshape(-1, HD)
        v = vi_ref[c * per : (c + 1) * per].reshape(-1, HD)
        s = lax.dot_general(q, k, dims, preferred_element_type=jnp.float32) * HD ** (-0.5)
        m_new = jnp.maximum(m, jnp.max(s, axis=1, keepdims=True))
        alpha = jnp.exp(m - m_new)
        e = jnp.exp(s - m_new)
        l = alpha * l + jnp.sum(e, axis=1, keepdims=True)
        acc = alpha * acc + jnp.dot(e.astype(jnp.bfloat16), v, preferred_element_type=jnp.float32)
        m = m_new
    o = acc * (1.0 / l)
    o_ref[...] = o.astype(o_ref.dtype).reshape(o_ref.shape)
    m_ref[...] = jnp.full(m_ref.shape, jnp.max(m), jnp.float32)


def attention(text_len, buf, rows, trows):
    src = buf.shape[0]
    img_len = src * rows
    txt_len = src * trows
    per = BQ // rows
    nq = src // per
    grid_spec = pltpu.PrefetchScalarGridSpec(
        num_scalar_prefetch=1,
        grid=(1, nq),
        in_specs=[
            pl.BlockSpec((per, rows, HD), lambda p, i, tl: (i, 0, 0)),
            pl.BlockSpec((src, trows, HD), lambda p, i, tl: (0, 3 * rows // trows, 0)),
            pl.BlockSpec((src, trows, HD), lambda p, i, tl: (0, 3 * rows // trows + 1, 0)),
            pl.BlockSpec((src, rows, HD), lambda p, i, tl: (0, 1, 0)),
            pl.BlockSpec((src, rows, HD), lambda p, i, tl: (0, 2, 0)),
        ],
        out_specs=[
            pl.BlockSpec((per, rows, HD), lambda p, i, tl: (i, 0, 0)),
            pl.BlockSpec((None, 8, 128), lambda p, i, tl: (i, 0, 0)),
        ],
    )
    cost = pl.CostEstimate(
        flops=4 * img_len * (img_len + txt_len) * HD,
        transcendentals=img_len * (img_len + txt_len),
        bytes_accessed=buf.size * 2 + img_len * HD * 2,
    )
    out, top = pl.pallas_call(
        attn_kernel,
        grid_spec=grid_spec,
        out_shape=[
            jax.ShapeDtypeStruct((src, rows, HD), jnp.bfloat16),
            jax.ShapeDtypeStruct((nq, 8, 128), jnp.float32),
        ],
        compiler_params=pltpu.CompilerParams(
            dimension_semantics=("arbitrary", "arbitrary"),
            vmem_limit_bytes=60 * 1024 * 1024,
        ),
        cost_estimate=cost,
    )(text_len, buf, buf, buf, buf, buf)
    return out, jnp.max(top)[None]


def shards(
    img_qkv,
    txt_kv,
    text_len,
    t_index,
    guidance,
    modulation,
    img_hidden,
    latents,
    proj_weight,
    final_weight,
):
    local_prompts = img_qkv.shape[1]
    img_dev = img_qkv.shape[2]
    txt_dev = txt_kv.shape[2]
    seq = lax.axis_size("seq")
    img_len = img_dev * seq
    outs = []
    maxes = []
    for p in range(local_prompts):
        joined = img_qkv[0, p].reshape(img_dev, 3, seq, HEADS // seq * HD)
        joined = joined.transpose(2, 1, 0, 3).reshape(seq, 3 * img_dev, HD)
        text_rows = txt_kv[0, p].reshape(txt_dev, 2, seq, HEADS // seq * HD)
        text_rows = text_rows.transpose(2, 1, 0, 3).reshape(seq, 2 * txt_dev, HD)
        buf = lax.all_to_all(
            jnp.concatenate([joined, text_rows], axis=1), "seq", 0, 0, tiled=True
        )
        head_rows, top = attention(text_len[p : p + 1], buf, img_dev, txt_dev)
        outs.append(lax.all_to_all(head_rows, "seq", 0, 0, tiled=True)[:, None])
        maxes.append(top)
    local_max = jnp.concatenate(maxes)
    weight = lax.all_gather(proj_weight, ("cfg", "req", "seq"), axis=0, tiled=True)
    weight = weight.reshape(seq, HEADS // seq * HD, weight.shape[1])
    mod_rows = modulation[0]
    velocities = []
    for p in range(local_prompts):
        projected = jnp.einsum(
            "htd,hdo->to", outs[p][:, 0], weight, preferred_element_type=jnp.float32
        )
        hidden = img_hidden[0, p].astype(jnp.float32) + mod_rows[p, 0][None, :] * projected
        average = jnp.mean(hidden, axis=1, keepdims=True)
        centred = hidden - average
        variance = jnp.mean(centred * centred, axis=1, keepdims=True)
        normed = (
            centred / jnp.sqrt(variance + norm_eps) * (1.0 + mod_rows[p, 1][None, :])
            + mod_rows[p, 2][None, :]
        ).astype(jnp.bfloat16)
        velocities.append(jnp.dot(normed, final_weight, preferred_element_type=jnp.float32))
    velocity = jnp.stack(velocities)
    half_chan = latents.shape[2]
    copy_pos = lax.axis_index("cfg")
    own_part = lax.dynamic_slice_in_dim(velocity, copy_pos * half_chan, half_chan, 2)
    other_part = lax.dynamic_slice_in_dim(velocity, (1 - copy_pos) * half_chan, half_chan, 2)
    partner = swapped(other_part, "cfg", 0)
    is_cond = copy_pos == 0
    cond_vel = jnp.where(is_cond, own_part, partner)
    uncond_vel = jnp.where(is_cond, partner, own_part)
    guided = uncond_vel + guidance[:, None, None] * (cond_vel - uncond_vel)
    square_sum = jnp.sum(guided * guided, axis=(1, 2))
    stats = jnp.concatenate([square_sum, local_max])
    gathered = lax.all_to_all(
        jnp.broadcast_to(stats[None], (seq, stats.shape[0])), "seq", 0, 0, tiled=True
    )
    total_sq = jnp.sum(gathered[:, :local_prompts], axis=0)
    global_max = jnp.max(gathered[:, local_prompts:], axis=0)
    vel_norm = jnp.sqrt(total_sq / (img_len * half_chan) + norm_eps)
    euler_step = sigma_of(t_index + 1) - sigma_of(t_index)
    advanced = latents + euler_step[:, None, None] * guided
    return (advanced, vel_norm.reshape(1, local_prompts), global_max.reshape(1, local_prompts))


def solution(mesh):
    return jax.shard_map(
        shards,
        mesh=mesh,
        in_specs=(
            P("cfg", "req", "seq", None),
            P("cfg", "req", "seq", None),
            P("req"),
            P("req"),
            P("req"),
            P("cfg", "req", None, None),
            P("cfg", "req", "seq", None),
            P("req", "seq", "cfg"),
            P(("cfg", "req", "seq"), None),
            P(),
        ),
        out_specs=(P("req", "seq", "cfg"), P("cfg", "req"), P("cfg", "req")),
        check_vma=False,
    )
```

```python
import functools
import math

import jax
import jax.numpy as jnp
from jax import lax
from jax.experimental import pallas as pl
from jax.experimental.pallas import tpu as pltpu
from jax.sharding import PartitionSpec as P

HEADS = 16
HD = 128
STEPS = 4
BQ = 1024
CK = 2048


time_shift = 1.15
norm_eps = 1e-06


def swapped(value, axis, stride):
    return lax.ppermute(value, axis, [(i, i ^ 1 << stride) for i in range(lax.axis_size(axis))])


def sigma_of(step_index):
    fraction = 1.0 - step_index.astype(jnp.float32) / STEPS
    lifted = fraction * math.exp(time_shift)
    return lifted / (lifted + 1.0 - fraction)


def attn_kernel(tl_ref, q_ref, kt_ref, vt_ref, ki_ref, vi_ref, o_ref, m_ref):
    dims = (((1,), (1,)), ((), ()))
    q = q_ref[...].reshape(-1, HD)
    st = lax.dot_general(q, kt_ref[...].reshape(-1, HD), dims, preferred_element_type=jnp.float32)
    st = st * HD ** (-0.5)
    col = lax.broadcasted_iota(jnp.int32, st.shape, 1)
    st = jnp.where(col < tl_ref[0], st, -jnp.inf)
    m = jnp.max(st, axis=1, keepdims=True)
    e = jnp.exp(st - m)
    l = jnp.sum(e, axis=1, keepdims=True)
    acc = jnp.dot(
        e.astype(jnp.bfloat16), vt_ref[...].reshape(-1, HD), preferred_element_type=jnp.float32
    )
    per = CK // ki_ref.shape[1]
    for c in range(ki_ref.shape[0] // per):
        k = ki_ref[c * per : (c + 1) * per].reshape(-1, HD)
        v = vi_ref[c * per : (c + 1) * per].reshape(-1, HD)
        s = lax.dot_general(q, k, dims, preferred_element_type=jnp.float32) * HD ** (-0.5)
        m_new = jnp.maximum(m, jnp.max(s, axis=1, keepdims=True))
        alpha = jnp.exp(m - m_new)
        e = jnp.exp(s - m_new)
        l = alpha * l + jnp.sum(e, axis=1, keepdims=True)
        acc = alpha * acc + jnp.dot(e.astype(jnp.bfloat16), v, preferred_element_type=jnp.float32)
        m = m_new
    o = acc * (1.0 / l)
    o_ref[...] = o.astype(o_ref.dtype).reshape(o_ref.shape)
    m_ref[...] = jnp.full(m_ref.shape, jnp.max(m), jnp.float32)


def attention(text_len, buf, rows, trows):
    src = buf.shape[0]
    img_len = src * rows
    txt_len = src * trows
    per = BQ // rows
    nq = src // per
    grid_spec = pltpu.PrefetchScalarGridSpec(
        num_scalar_prefetch=1,
        grid=(1, nq),
        in_specs=[
            pl.BlockSpec((per, rows, HD), lambda p, i, tl: (i, 0, 0)),
            pl.BlockSpec((src, trows, HD), lambda p, i, tl: (0, 3 * rows // trows, 0)),
            pl.BlockSpec((src, trows, HD), lambda p, i, tl: (0, 3 * rows // trows + 1, 0)),
            pl.BlockSpec((src, rows, HD), lambda p, i, tl: (0, 1, 0)),
            pl.BlockSpec((src, rows, HD), lambda p, i, tl: (0, 2, 0)),
        ],
        out_specs=[
            pl.BlockSpec((per, rows, HD), lambda p, i, tl: (i, 0, 0)),
            pl.BlockSpec((None, 8, 128), lambda p, i, tl: (i, 0, 0)),
        ],
    )
    cost = pl.CostEstimate(
        flops=4 * img_len * (img_len + txt_len) * HD,
        transcendentals=img_len * (img_len + txt_len),
        bytes_accessed=buf.size * 2 + img_len * HD * 2,
    )
    out, top = pl.pallas_call(
        attn_kernel,
        grid_spec=grid_spec,
        out_shape=[
            jax.ShapeDtypeStruct((src, rows, HD), jnp.bfloat16),
            jax.ShapeDtypeStruct((nq, 8, 128), jnp.float32),
        ],
        compiler_params=pltpu.CompilerParams(
            dimension_semantics=("arbitrary", "arbitrary"),
            vmem_limit_bytes=60 * 1024 * 1024,
        ),
        cost_estimate=cost,
    )(text_len, buf, buf, buf, buf, buf)
    return out, jnp.max(top)[None]


def shards(
    img_qkv,
    txt_kv,
    text_len,
    t_index,
    guidance,
    modulation,
    img_hidden,
    latents,
    proj_weight,
    final_weight,
):
    local_prompts = img_qkv.shape[1]
    img_dev = img_qkv.shape[2]
    txt_dev = txt_kv.shape[2]
    seq = lax.axis_size("seq")
    img_len = img_dev * seq
    outs = []
    maxes = []
    for p in range(local_prompts):
        joined = img_qkv[0, p].reshape(img_dev, 3, seq, HEADS // seq * HD)
        joined = joined.transpose(2, 1, 0, 3).reshape(seq, 3 * img_dev, HD)
        text_rows = txt_kv[0, p].reshape(txt_dev, 2, seq, HEADS // seq * HD)
        text_rows = text_rows.transpose(2, 1, 0, 3).reshape(seq, 2 * txt_dev, HD)
        buf = lax.all_to_all(
            jnp.concatenate([joined, text_rows], axis=1), "seq", 0, 0, tiled=True
        )
        head_rows, top = attention(text_len[p : p + 1], buf, img_dev, txt_dev)
        outs.append(lax.all_to_all(head_rows, "seq", 0, 0, tiled=True)[:, None])
        maxes.append(top)
    local_max = jnp.concatenate(maxes)
    weight = lax.all_gather(proj_weight, ("cfg", "req", "seq"), axis=0, tiled=True)
    weight = weight.reshape(seq, HEADS // seq * HD, weight.shape[1])
    mod_rows = modulation[0]
    velocities = []
    for p in range(local_prompts):
        projected = jnp.einsum(
            "htd,hdo->to", outs[p][:, 0], weight, preferred_element_type=jnp.float32
        )
        hidden = img_hidden[0, p].astype(jnp.float32) + mod_rows[p, 0][None, :] * projected
        average = jnp.mean(hidden, axis=1, keepdims=True)
        centred = hidden - average
        variance = jnp.mean(centred * centred, axis=1, keepdims=True)
        normed = (
            centred / jnp.sqrt(variance + norm_eps) * (1.0 + mod_rows[p, 1][None, :])
            + mod_rows[p, 2][None, :]
        ).astype(jnp.bfloat16)
        velocities.append(jnp.dot(normed, final_weight, preferred_element_type=jnp.float32))
    velocity = jnp.stack(velocities)
    half_chan = latents.shape[2]
    copy_pos = lax.axis_index("cfg")
    own_part = lax.dynamic_slice_in_dim(velocity, copy_pos * half_chan, half_chan, 2)
    other_part = lax.dynamic_slice_in_dim(velocity, (1 - copy_pos) * half_chan, half_chan, 2)
    partner = swapped(other_part, "cfg", 0)
    is_cond = copy_pos == 0
    cond_vel = jnp.where(is_cond, own_part, partner)
    uncond_vel = jnp.where(is_cond, partner, own_part)
    guided = uncond_vel + guidance[:, None, None] * (cond_vel - uncond_vel)
    square_sum = jnp.sum(guided * guided, axis=(1, 2))
    stats = jnp.concatenate([square_sum, local_max])
    gathered = lax.all_to_all(
        jnp.broadcast_to(stats[None], (seq, stats.shape[0])), "seq", 0, 0, tiled=True
    )
    total_sq = jnp.sum(gathered[:, :local_prompts], axis=0)
    global_max = jnp.max(gathered[:, local_prompts:], axis=0)
    vel_norm = jnp.sqrt(total_sq / (img_len * half_chan) + norm_eps)
    euler_step = sigma_of(t_index + 1) - sigma_of(t_index)
    advanced = latents + euler_step[:, None, None] * guided
    return (advanced, vel_norm.reshape(1, local_prompts), global_max.reshape(1, local_prompts))


def solution(mesh):
    return jax.shard_map(
        shards,
        mesh=mesh,
        in_specs=(
            P("cfg", "req", "seq", None),
            P("cfg", "req", "seq", None),
            P("req"),
            P("req"),
            P("req"),
            P("cfg", "req", None, None),
            P("cfg", "req", "seq", None),
            P("req", "seq", "cfg"),
            P(("cfg", "req", "seq"), None),
            P(),
        ),
        out_specs=(P("req", "seq", "cfg"), P("cfg", "req"), P("cfg", "req")),
        check_vma=False,
    )
```
